32 devices in a mesh: dp: 4 (over z), ctx: 2 (over y), fsdp: 4 (over x, core).
Axes of the slice: x: 2, y: 2, z: 4, core: 2. Of those that a mesh axis runs over, the one named last changes fastest.
Arguments:
- inputs: bfloat16 [16, 256, 1088], P(('dp', 'fsdp'), 'ctx'), may hold values from -6 to 6
- pair_table: int32 [2, 2], replicated, may hold values from 0 to 3, as said below
- first_gain: float32 [1088], replicated, may hold values from 0.1 to 1.9
- first_shift: float32 [1088], replicated, may hold values from -4 to 4
- proj_weight: bfloat16 [1088, 3264], P('fsdp'), may hold values from -8 to 8
- query_bias: float32 [1088], replicated, may hold values from -4 to 4
- value_bias: float32 [1088], replicated, may hold values from -4 to 4
- mix_weight: bfloat16 [1088, 1088], P('fsdp'), may hold values from -2 to 2
- mix_bias: float32 [1088], replicated, may hold values from -4 to 4
- second_gain: float32 [1088], replicated, may hold values from 0.1 to 1.9
- second_shift: float32 [1088], replicated, may hold values from -4 to 4
- up_weight: bfloat16 [1088, 4352], P('fsdp'), may hold values from -0.1875 to 0.1875
- up_bias: float32 [4352], replicated, may hold values from -4 to 4
- down_weight: bfloat16 [4352, 1088], P('fsdp'), may hold values from -0.1875 to 0.1875
- down_bias: float32 [1088], replicated, may hold values from -4 to 4
- output_grad: float32 [16, 256, 1088], P(('dp', 'fsdp'), 'ctx'), may hold values from -6 to 6
Outputs:
- outputs: float32 [16, 256, 1088], P(('dp', 'fsdp'), 'ctx')
- input_grad: float32 [16, 256, 1088], P(('dp', 'fsdp'), 'ctx')
- first_gain_grad: float32 [1088], replicated
- first_shift_grad: float32 [1088], replicated
- proj_weight_grad: float32 [1088, 3264], P(('dp', 'fsdp'), 'ctx')
- query_bias_grad: float32 [1088], replicated
- value_bias_grad: float32 [1088], replicated
- mix_weight_grad: float32 [1088, 1088], P(('dp', 'fsdp'), 'ctx')
- mix_bias_grad: float32 [1088], replicated
- second_gain_grad: float32 [1088], replicated
- second_shift_grad: float32 [1088], replicated
- up_weight_grad: float32 [1088, 4352], P(('dp', 'fsdp'), 'ctx')
- up_bias_grad: float32 [4352], replicated
- down_weight_grad: float32 [4352, 1088], P(('dp', 'fsdp'), 'ctx')
- down_bias_grad: float32 [1088], replicated
The draws below stay inside these ranges and needn't reach their ends.
Inputs may be any that keep to these rules, and one draw needn't show every extreme that they name: `pair_table`: each row holds one block b below 2 and its mirror 2 * 2 - 1 - b, in either order; every block of a sequence appears once in the table.
All inputs are finite; a program needn't handle non-finite values.
Results may differ from the reference program's by a relative error of at most 0.012.
The reference program's roundings to bfloat16 on the way count: a program that leaves them out, or rounds other values in their place, can miss the bound.
Values may be sent and summed in bfloat16 or wider, within the bound.
No kernel may reach another device: no remote copies, remote signals or barrier semaphores. Data moves between devices by JAX's collectives and lax.ppermute only.
A program may use at most 256 MiB of HBM per device.

```python
import math
import jax
import jax.numpy as jnp
from jax import lax

D = 1088
HEADS = 17
HEAD_DIM = 64
FF = 4352
BLK = 64
SEQS = 16
SEQLEN = 256


def draw_inputs(key, part):
    key_first = jax.random.fold_in(key, 0)
    entries = jax.random.normal(key_first, (SEQS, SEQLEN, D), jnp.float32)
    return jnp.clip(entries, -6.0, 6.0).astype(jnp.bfloat16)


def draw_pair_table(key, part):
    cycle_size = SEQLEN // (2 * BLK)
    key_order, key_flip = jax.random.split(key)
    lower = jax.random.permutation(key_order, cycle_size).astype(jnp.int32)
    mirror = 2 * cycle_size - 1 - lower
    flipped = jax.random.randint(key_flip, (cycle_size,), 0, 2) == 1
    first = jnp.where(flipped, mirror, lower)
    second = jnp.where(flipped, lower, mirror)
    return jnp.stack([first, second], axis=1).astype(jnp.int32)


def draw_proj_weight(key, part):
    key_first = jax.random.fold_in(key, 0)
    entries = jnp.clip(jax.random.normal(key_first, (D, 3 * D), jnp.float32), -6.0, 6.0) * D ** (-0.5)
    return jnp.clip(entries, -8.0, 8.0).astype(jnp.bfloat16)


def block_scale(rng, dims, pieces, low, high):
    factor_of = 1.0
    for dim, shards_of in pieces:
        heights = jax.random.uniform(jax.random.fold_in(jax.random.fold_in(rng, 6), dim), (shards_of,), jnp.float32, low / len(pieces), high / len(pieces))
        factor_of = factor_of * jnp.repeat(jnp.exp(heights), dims[dim] // shards_of).reshape((-1,) + (1,) * (len(dims) - 1 - dim))
    return factor_of


def noise(key, dims, scale, bound, shards=(), held_as=jnp.bfloat16):
    level = block_scale(key, dims, shards, -0.22, 0.18) if shards else 1.0
    drawn = jax.random.normal(key, dims, jnp.float32) * scale * level
    return jnp.minimum(jnp.maximum(drawn, -bound), bound).astype(held_as)


def setup_inputs(seed: int = 0) -> dict:
    arg_keys = jax.random.split(jax.random.key(seed), 17)
    return {
        "inputs": draw_inputs(jax.random.fold_in(arg_keys[16], 71), 0),
        "pair_table": draw_pair_table(jax.random.fold_in(arg_keys[16], 71), 0),
        "first_gain": jnp.clip(1.0 + 0.18 * jax.random.normal(arg_keys[2], (D,), jnp.float32), 0.1, 1.9),
        "first_shift": noise(arg_keys[3], (D,), 0.5, 4.0, (), jnp.float32),
        "proj_weight": draw_proj_weight(jax.random.fold_in(arg_keys[16], 71), 0),
        "query_bias": noise(arg_keys[5], (D,), 1.0, 4.0, (), jnp.float32),
        "value_bias": noise(arg_keys[6], (D,), 0.5, 4.0, (), jnp.float32),
        "mix_weight": noise(arg_keys[7], (D, D), (max(1, 2 * D // SEQLEN)) ** -0.5, 2.0, ((0, 4),)),
        "mix_bias": noise(arg_keys[8], (D,), 0.5, 4.0, (), jnp.float32),
        "second_gain": jnp.clip(1.0 + 0.18 * jax.random.normal(arg_keys[9], (D,), jnp.float32), 0.1, 1.9),
        "second_shift": noise(arg_keys[10], (D,), 0.5, 4.0, (), jnp.float32),
        "up_weight": noise(arg_keys[11], (D, FF), D ** -0.5, 0.1875, ((0, 4),)),
        "up_bias": noise(arg_keys[12], (FF,), 0.5, 4.0, (), jnp.float32),
        "down_weight": noise(arg_keys[13], (FF, D), (FF // 4) ** -0.5, 0.1875, ((0, 4),)),
        "down_bias": noise(arg_keys[14], (D,), 0.5, 4.0, (), jnp.float32),
        "output_grad": noise(arg_keys[15], (SEQS, SEQLEN, D), 1.0, 6.0, ((0, 16), (1, 2)), jnp.float32),
    }


EPSILON = 1e-05
NEGATIVE_FILL = -1e+30

def normalize(values, gain, shift):
    center = values - lax.optimization_barrier(jnp.mean(values, axis=-1, keepdims=True))
    inverse = lax.rsqrt(lax.optimization_barrier(jnp.mean(center * center, axis=-1, keepdims=True)) + EPSILON)
    normed = center * inverse
    return (normed, inverse, normed * gain + shift)

def normalize_back(incoming, normed, inverse, gain):
    gain_grad = lax.optimization_barrier(jnp.sum(incoming * normed, axis=0))
    shift_grad = lax.optimization_barrier(jnp.sum(incoming, axis=0))
    scaled = incoming * gain
    result = inverse * (scaled - lax.optimization_barrier(jnp.mean(scaled, axis=-1, keepdims=True)) - normed * lax.optimization_barrier(jnp.mean(scaled * normed, axis=-1, keepdims=True)))
    return (result, gain_grad, shift_grad)

def gelu_pair(preact):
    normal_cdf = 0.5 * (1.0 + lax.erf(preact * (1.0 / math.sqrt(2.0))))
    density = jnp.exp(-0.5 * preact * preact) * (1.0 / math.sqrt(2.0 * math.pi))
    return (preact * normal_cdf, normal_cdf + preact * density)

def rounded(values):
    return lax.optimization_barrier(values.astype(jnp.bfloat16))

def reference(inputs, pair_table, first_gain, first_shift, proj_weight, query_bias, value_bias, mix_weight, mix_bias, second_gain, second_shift, up_weight, up_bias, down_weight, down_bias, output_grad):
    offsets = jnp.arange(BLK, dtype=jnp.int32)
    positions = (pair_table.astype(jnp.int32)[:, :, None] * BLK + offsets[None, None, :]).reshape(-1)
    visible = positions[:, None] >= positions[None, :]
    scale = 1.0 / math.sqrt(HEAD_DIM)
    length = positions.shape[0]

    def split_heads(values):
        return values.astype(jnp.float32).reshape(length, HEADS, HEAD_DIM)

    def one_sequence(totals, pair):
        tokens, incoming = pair
        x_float = tokens.astype(jnp.float32)
        normed1, inverse1, scaled_first = normalize(x_float, first_gain, first_shift)
        first_in = rounded(scaled_first)
        projected = jnp.dot(first_in, proj_weight, preferred_element_type=jnp.float32)
        query = rounded(projected[:, :D] + query_bias)
        keys = rounded(projected[:, D:2 * D])
        values = rounded(projected[:, 2 * D:] + value_bias)
        query_heads = split_heads(query)
        key_heads = split_heads(keys)
        value_heads = split_heads(values)
        scores = jnp.einsum('qhd,khd->hqk', query_heads, key_heads) * scale
        masked = jnp.where(visible[None], scores, NEGATIVE_FILL)
        row_top = lax.optimization_barrier(jnp.max(masked, axis=2, keepdims=True))
        log_total = row_top + jnp.log(lax.optimization_barrier(jnp.sum(jnp.where(visible[None], jnp.exp(masked - row_top), 0.0), axis=2, keepdims=True)))
        probs_exact = jnp.where(visible[None], jnp.exp(masked - log_total), 0.0)
        probs_float = rounded(probs_exact).astype(jnp.float32)
        attended = rounded(jnp.einsum('hqk,khd->qhd', probs_float, value_heads).reshape(length, D))
        residual = x_float + jnp.dot(attended, mix_weight, preferred_element_type=jnp.float32) + mix_bias
        normed2, inverse2, scaled_second = normalize(residual, second_gain, second_shift)
        second_in = rounded(scaled_second)
        up_pre = jnp.dot(second_in, up_weight, preferred_element_type=jnp.float32) + up_bias
        activation, slope = gelu_pair(up_pre)
        activation_half = rounded(activation)
        result = residual + jnp.dot(activation_half, down_weight, preferred_element_type=jnp.float32) + down_bias
        upstream = rounded(incoming)
        down_weight_grad = jnp.dot(activation_half.T, upstream, preferred_element_type=jnp.float32)
        up_grad = jnp.dot(upstream, down_weight.T, preferred_element_type=jnp.float32) * slope
        up_half = rounded(up_grad)
        up_weight_grad = jnp.dot(second_in.T, up_half, preferred_element_type=jnp.float32)
        second_back = jnp.dot(up_half, up_weight.T, preferred_element_type=jnp.float32)
        residual_part, second_gain_grad, second_shift_grad = normalize_back(second_back, normed2, inverse2, second_gain)
        residual_grad = incoming + residual_part
        residual_half = rounded(residual_grad)
        mix_weight_grad = jnp.dot(attended.T, residual_half, preferred_element_type=jnp.float32)
        attended_grad = rounded(jnp.dot(residual_half, mix_weight.T, preferred_element_type=jnp.float32))
        grad_heads = split_heads(attended_grad)
        attended_heads = split_heads(attended)
        delta = jnp.einsum('qhd,qhd->hq', grad_heads, attended_heads)
        prob_grad = jnp.einsum('qhd,khd->hqk', grad_heads, value_heads)
        score_grad = rounded(probs_exact * (prob_grad - delta[:, :, None]) * scale).astype(jnp.float32)
        query_grad = jnp.einsum('hqk,khd->qhd', score_grad, key_heads).reshape(length, D)
        key_grad = jnp.einsum('hqk,qhd->khd', score_grad, query_heads).reshape(length, D)
        value_grad = jnp.einsum('hqk,qhd->khd', probs_float, grad_heads).reshape(length, D)
        proj_half = rounded(jnp.concatenate([query_grad, key_grad, value_grad], axis=1))
        proj_weight_grad = jnp.dot(first_in.T, proj_half, preferred_element_type=jnp.float32)
        first_back = jnp.dot(proj_half, proj_weight.T, preferred_element_type=jnp.float32)
        input_part, first_gain_grad, first_shift_grad = normalize_back(first_back, normed1, inverse1, first_gain)
        input_grad = residual_grad + input_part
        terms = (first_gain_grad, first_shift_grad, proj_weight_grad, lax.optimization_barrier(jnp.sum(query_grad, axis=0)), lax.optimization_barrier(jnp.sum(value_grad, axis=0)), mix_weight_grad, lax.optimization_barrier(jnp.sum(residual_grad, axis=0)), second_gain_grad, second_shift_grad, up_weight_grad, lax.optimization_barrier(jnp.sum(up_grad, axis=0)), down_weight_grad, lax.optimization_barrier(jnp.sum(incoming, axis=0)))
        return (jax.tree.map(jnp.add, totals, terms), (result, input_grad))
    zeros = (jnp.zeros((D,), jnp.float32), jnp.zeros((D,), jnp.float32), jnp.zeros((D, 3 * D), jnp.float32), jnp.zeros((D,), jnp.float32), jnp.zeros((D,), jnp.float32), jnp.zeros((D, D), jnp.float32), jnp.zeros((D,), jnp.float32), jnp.zeros((D,), jnp.float32), jnp.zeros((D,), jnp.float32), jnp.zeros((D, FF), jnp.float32), jnp.zeros((FF,), jnp.float32), jnp.zeros((FF, D), jnp.float32), jnp.zeros((D,), jnp.float32))
    totals, stacked = lax.scan(one_sequence, zeros, (inputs, output_grad))
    outputs, input_grad = stacked
    return (outputs, input_grad, totals[0], totals[1], totals[2], totals[3], totals[4], totals[5], totals[6], totals[7], totals[8], totals[9], totals[10], totals[11], totals[12])
```

```python
import math

import jax
import jax.numpy as jnp
from jax import lax
from jax.sharding import PartitionSpec as P

D = 1088
HEADS = 17
HEAD_DIM = 64
BLK = 64


EPSILON = 1e-05
NEGATIVE_FILL = -1e30


def normalize(values, gain, shift):
    center = values - jnp.mean(values, axis=-1, keepdims=True)
    inverse = lax.rsqrt(jnp.mean(center * center, axis=-1, keepdims=True) + EPSILON)
    normed = center * inverse
    return (normed, inverse, normed * gain + shift)


def normalize_back(incoming, normed, inverse, gain):
    gain_grad = jnp.sum(incoming * normed, axis=0)
    shift_grad = jnp.sum(incoming, axis=0)
    scaled = incoming * gain
    result = inverse * (
        scaled
        - jnp.mean(scaled, axis=-1, keepdims=True)
        - normed * jnp.mean(scaled * normed, axis=-1, keepdims=True)
    )
    return (result, gain_grad, shift_grad)


def gelu_pair(preact):
    normal_cdf = 0.5 * (1.0 + lax.erf(preact * (1.0 / math.sqrt(2.0))))
    density = jnp.exp(-0.5 * preact * preact) * (1.0 / math.sqrt(2.0 * math.pi))
    return (preact * normal_cdf, normal_cdf + preact * density)


def contract_rows(left, right):
    return lax.dot_general(
        left, right, (((0,), (0,)), ((), ())), preferred_element_type=jnp.float32
    )


def contract_cols(left, right):
    return lax.dot_general(
        left, right, (((1,), (1,)), ((), ())), preferred_element_type=jnp.float32
    )


def core_swap(array):
    return lax.ppermute(array, "fsdp", [(i, i ^ 1) for i in range(4)])


def chip_swap(array):
    return lax.ppermute(array, "fsdp", [(i, i ^ 2) for i in range(4)])


def gather_group(array):
    across = chip_swap(array)
    return jnp.concatenate([array, core_swap(array), across, core_swap(across)], axis=0)


def scatter_group(partial):
    own, near, far, diagonal = jnp.split(partial, 4, axis=0)
    received = core_swap(jnp.concatenate([near, diagonal], axis=0))
    count = own.shape[0]
    sent = (far + received[count:]).astype(jnp.bfloat16)
    return own + received[:count] + chip_swap(sent).astype(jnp.float32)


def exchange_columns(array, rank):
    width = array.shape[1] // 4
    pieces = []
    for step in range(4):
        piece = lax.dynamic_slice_in_dim(array, (rank ^ step) * width, width, 1)
        if step:
            piece = lax.ppermute(piece, "fsdp", [(i, i ^ step) for i in range(4)])
        pieces.append(piece)
    return pieces


def line_reduce(parts, rank, count, axis):
    final = lax.dynamic_index_in_dim(parts, rank, 0, keepdims=False)
    if count == 1:
        return final
    for direction in (1, -1):
        place = rank if direction == 1 else count - 1 - rank
        received = None
        for step in range(count - 1):
            ahead = jnp.clip(count - 1 - step + place, 0, count - 1)
            shard = ahead if direction == 1 else count - 1 - ahead
            value = lax.dynamic_index_in_dim(parts, shard, 0, keepdims=False)
            if received is not None:
                value = value + received.astype(jnp.float32)
            pairs = []
            for i in range(step + 1):
                pairs.append((i, i + 1) if direction == 1 else (count - 1 - i, count - 2 - i))
            received = lax.ppermute(value.astype(jnp.bfloat16), axis, pairs)
        final = final + received.astype(jnp.float32)
    return final


def all_sum(array, mesh_axes):
    for axis, count in mesh_axes:
        bit = 1
        while bit < count:
            array = array + lax.ppermute(array, axis, [(i, i ^ bit) for i in range(count)])
            bit *= 2
    return array


def head_major(values):
    count = values.shape[0]
    return jnp.transpose(values.reshape(count, HEADS, HEAD_DIM), (1, 0, 2))


def row_major(values):
    count = values.shape[1]
    return jnp.transpose(values, (1, 0, 2)).reshape(count, HEADS * HEAD_DIM)


def make_body(mesh):
    n_dp, n_ctx, n_fsdp = mesh.shape["dp"], mesh.shape["ctx"], mesh.shape["fsdp"]
    paired = n_ctx == 2

    def gather_weight(shard, rank, split):
        rows, width = shard.shape
        near = core_swap(shard)
        out = jnp.zeros((4 * rows, width), shard.dtype)
        if split and paired:
            side = lax.axis_index("ctx")
            half = rows // 2
            piece = chip_swap(lax.dynamic_slice_in_dim(shard, side * half, half, 0))
            other = lax.ppermute(piece, "ctx", [(0, 1), (1, 0)])
            parts = [(piece, 2, side * half), (other, 2, (1 - side) * half)]
            parts += [(core_swap(piece), 3, side * half), (core_swap(other), 3, (1 - side) * half)]
        else:
            across = chip_swap(shard)
            parts = [(across, 2, 0), (core_swap(across), 3, 0)]
        for value, step, offset in [(shard, 0, 0), (near, 1, 0)] + parts:
            out = lax.dynamic_update_slice_in_dim(out, value, (rank ^ step) * rows + offset, 0)
        return out

    def own_columns(left, right, rank_dp, rank_ctx, rank):
        rows, width = left.shape[1], right.shape[1]
        share = rows // (4 * n_dp)
        if not paired:
            product = contract_rows(left, right).reshape(n_dp, 4, share, width)
            product = lax.all_to_all(product, "fsdp", 1, 3, tiled=True)
            product = product.reshape(n_dp * share, 4 * width)
            product = lax.psum_scatter(product, "dp", scatter_dimension=0, tiled=True)
            return lax.psum_scatter(product, "ctx", scatter_dimension=1, tiled=True)
        sides = left.reshape(-1, n_dp, 2, 2 * share)
        low, high = (sides[:, :, i].reshape(-1, rows // 2) for i in range(2))
        kept = jnp.where(rank_ctx == 0, low, high)
        given = jnp.where(rank_ctx == 0, high, low)
        received = lax.ppermute(
            contract_rows(given, right).astype(jnp.bfloat16), "ctx", [(0, 1), (1, 0)]
        )
        total = contract_rows(kept, right) + received.astype(jnp.float32)
        total = line_reduce(total.reshape(n_dp, 2 * share, width), rank_dp, n_dp, "dp")
        total = total.astype(jnp.bfloat16)
        core = rank % 2
        pieces = []
        for step in range(2):
            pairs = []
            for side in range(2):
                for source in range(4):
                    target = 2 * side + (source % 2 ^ step)
                    pairs.append((4 * side + source, 4 * (source // 2) + target))
            piece = lax.dynamic_slice_in_dim(total, (core ^ step) * share, share, 0)
            pieces.append(lax.ppermute(piece, ("ctx", "fsdp"), pairs).astype(jnp.float32))
        return jnp.where(
            core == 0, jnp.concatenate(pieces, axis=1), jnp.concatenate(pieces[::-1], axis=1)
        )

    def own_rows(left, right, rank_dp, rank_ctx, rank):
        rows, width = left.shape[1], right.shape[1]
        if not (paired and n_dp == 4):
            whole = jnp.zeros((4 * rows, width), jnp.float32)
            whole = lax.dynamic_update_slice_in_dim(
                whole, contract_rows(left, right), rank * rows, 0
            )
            whole = lax.psum_scatter(whole, ("dp", "fsdp"), scatter_dimension=0, tiled=True)
            return lax.psum_scatter(whole, "ctx", scatter_dimension=1, tiled=True)
        low, high = right[:, : width // 2], right[:, width // 2 :]
        kept = jnp.where(rank_ctx == 0, low, high)
        given = jnp.where(rank_ctx == 0, high, low)
        received = lax.ppermute(
            contract_rows(left, given).astype(jnp.bfloat16), "ctx", [(0, 1), (1, 0)]
        )
        total = contract_rows(left, kept) + received.astype(jnp.float32)
        total = line_reduce(total.reshape(4, rows // 4, width // 2), rank_dp, n_dp, "dp")
        pairs = [(4 * i + j, 4 * j + i) for i in range(4) for j in range(4)]
        return lax.ppermute(total.astype(jnp.bfloat16), ("dp", "fsdp"), pairs).astype(jnp.float32)

    def body(
        inputs,
        pair_table,
        first_gain,
        first_shift,
        proj_weight,
        query_bias,
        value_bias,
        mix_weight,
        mix_bias,
        second_gain,
        second_shift,
        up_weight,
        up_bias,
        down_weight,
        down_bias,
        output_grad,
    ):
        tokens = inputs[0]
        count = tokens.shape[0]
        incoming = output_grad[0]
        scale = 1.0 / math.sqrt(HEAD_DIM)
        rank_dp, rank_ctx = lax.axis_index("dp"), lax.axis_index("ctx")
        rank = lax.axis_index("fsdp")
        ranks = (rank_dp, rank_ctx, rank)

        shifts = range(1, n_ctx)
        all_tokens = jnp.concatenate(
            [tokens]
            + [lax.ppermute(tokens, "ctx", [(i, (i - s) % n_ctx) for i in range(n_ctx)]) for s in shifts],
            axis=0,
        )
        offsets = jnp.arange(BLK, dtype=jnp.int32)
        order = (rank_ctx + jnp.arange(n_ctx, dtype=jnp.int32)) % n_ctx
        key_pos = (pair_table[order][:, :, None] * BLK + offsets[None, None, :]).reshape(-1)
        query_pos = key_pos[:count]
        visible = query_pos[:, None] >= key_pos[None, :]

        full_proj = gather_weight(proj_weight, rank, True)
        full_mix = gather_weight(mix_weight, rank, False)
        upstream = incoming.astype(jnp.bfloat16)
        hidden_up = jnp.zeros((D, up_weight.shape[1] // 4), up_weight.dtype)
        for step, piece in enumerate(exchange_columns(up_weight, rank)):
            hidden_up = lax.dynamic_update_slice_in_dim(
                hidden_up, piece, (rank ^ step) * piece.shape[0], 0
            )
        hidden = hidden_up.shape[1]
        hidden_bias = lax.dynamic_slice_in_dim(up_bias, rank * hidden, hidden, 0)

        x_all = all_tokens.astype(jnp.float32)
        normed_all, inverse_all, scaled_all = normalize(x_all, first_gain, first_shift)
        first_all = scaled_all.astype(jnp.bfloat16)
        x_float, normed1, inverse1 = x_all[:count], normed_all[:count], inverse_all[:count]
        first_in = first_all[:count]
        projected = jnp.dot(first_all, full_proj, preferred_element_type=jnp.float32)
        query = (projected[:count, :D] + query_bias).astype(jnp.bfloat16)
        keys = projected[:, D : 2 * D].astype(jnp.bfloat16)
        values = (projected[:, 2 * D :] + value_bias).astype(jnp.bfloat16)
        query_heads = head_major(query)
        key_heads = head_major(keys)
        value_heads = head_major(values)
        scores = (
            jnp.einsum("hqd,hkd->hqk", query_heads, key_heads, preferred_element_type=jnp.float32)
            * scale
        )
        masked = jnp.where(visible[None], scores, NEGATIVE_FILL)
        row_top = jnp.max(masked, axis=2, keepdims=True)
        log_total = row_top + jnp.log(
            jnp.sum(jnp.where(visible[None], jnp.exp(masked - row_top), 0.0), axis=2, keepdims=True)
        )
        probs_exact = jnp.where(visible[None], jnp.exp(masked - log_total), 0.0)
        probs_half = probs_exact.astype(jnp.bfloat16)
        attended_heads = jnp.einsum(
            "hqk,hkd->hqd", probs_half, value_heads, preferred_element_type=jnp.float32
        ).astype(jnp.bfloat16)
        attended = row_major(attended_heads)
        residual = (
            x_float + jnp.dot(attended, full_mix, preferred_element_type=jnp.float32) + mix_bias
        )
        normed2, inverse2, scaled_second = normalize(residual, second_gain, second_shift)
        second_in = scaled_second.astype(jnp.bfloat16)

        group_upstream = gather_group(upstream)
        group_second = gather_group(second_in)
        up_pre = jnp.dot(group_second, hidden_up, preferred_element_type=jnp.float32) + hidden_bias
        activation, slope = gelu_pair(up_pre)
        activation_half = activation.astype(jnp.bfloat16)
        up_grad = contract_cols(group_upstream, down_weight) * slope
        up_half = up_grad.astype(jnp.bfloat16)
        second_back = scatter_group(contract_cols(up_half, hidden_up))
        outputs = (
            residual
            + scatter_group(jnp.dot(activation_half, down_weight, preferred_element_type=jnp.float32))
            + down_bias
        )
        down_share = own_rows(activation_half, group_upstream, *ranks)
        up_share = own_columns(group_second, up_half, *ranks)

        residual_part, second_gain_part, second_shift_part = normalize_back(
            second_back, normed2, inverse2, second_gain
        )
        residual_grad = incoming + residual_part
        residual_half = residual_grad.astype(jnp.bfloat16)
        mix_share = own_columns(
            gather_group(attended),
            jnp.concatenate(exchange_columns(residual_half, rank), axis=0),
            *ranks,
        )
        attended_grad = contract_cols(residual_half, full_mix).astype(jnp.bfloat16)
        grad_heads = head_major(attended_grad)
        delta = jnp.einsum(
            "hqd,hqd->hq", grad_heads, attended_heads, preferred_element_type=jnp.float32
        )
        prob_grad = jnp.einsum(
            "hqd,hkd->hqk", grad_heads, value_heads, preferred_element_type=jnp.float32
        )
        score_grad = (probs_exact * (prob_grad - delta[:, :, None]) * scale).astype(jnp.bfloat16)
        query_grad = row_major(
            jnp.einsum("hqk,hkd->hqd", score_grad, key_heads, preferred_element_type=jnp.float32)
        )
        key_part = row_major(
            jnp.einsum("hqk,hqd->hkd", score_grad, query_heads, preferred_element_type=jnp.float32)
        )
        value_part = row_major(
            jnp.einsum("hqk,hqd->hkd", probs_half, grad_heads, preferred_element_type=jnp.float32)
        )
        parts = jnp.concatenate([key_part, value_part], axis=1).reshape(n_ctx, count, 2 * D)
        key_value_grad = parts[0]
        for s in shifts:
            key_value_grad = key_value_grad + lax.ppermute(
                parts[s].astype(jnp.bfloat16), "ctx", [(i, (i + s) % n_ctx) for i in range(n_ctx)]
            ).astype(jnp.float32)
        proj_grad = jnp.concatenate([query_grad, key_value_grad], axis=1)
        proj_half = proj_grad.astype(jnp.bfloat16)
        proj_share = own_columns(
            gather_group(first_in),
            jnp.concatenate(exchange_columns(proj_half, rank), axis=0),
            *ranks,
        )
        first_back = contract_cols(proj_half, full_proj)
        input_part, first_gain_part, first_shift_part = normalize_back(
            first_back, normed1, inverse1, first_gain
        )
        input_grad = residual_grad + input_part

        axes = (("fsdp", n_fsdp), ("ctx", n_ctx), ("dp", n_dp))
        up_bias_part = lax.dynamic_update_slice_in_dim(
            jnp.zeros(up_bias.shape, jnp.float32), jnp.sum(up_grad, axis=0), rank * hidden, 0
        )
        early = all_sum(
            jnp.concatenate(
                [
                    jnp.sum(residual_grad, axis=0),
                    second_gain_part,
                    second_shift_part,
                    jnp.sum(incoming, axis=0),
                    up_bias_part,
                ]
            ),
            axes,
        )
        late = all_sum(
            jnp.concatenate(
                [
                    first_gain_part,
                    first_shift_part,
                    jnp.sum(query_grad, axis=0),
                    jnp.sum(key_value_grad[:, D:], axis=0),
                ]
            ),
            axes,
        )
        return (
            outputs[None],
            input_grad[None],
            late[:D],
            late[D : 2 * D],
            proj_share,
            late[2 * D : 3 * D],
            late[3 * D :],
            mix_share,
            early[:D],
            early[D : 2 * D],
            early[2 * D : 3 * D],
            up_share,
            early[4 * D :],
            down_share,
            early[3 * D : 4 * D],
        )

    return body


def solution(mesh):
    in_specs = (
        P(("dp", "fsdp"), "ctx", None),
        P(),
        P(),
        P(),
        P("fsdp", None),
        P(),
        P(),
        P("fsdp", None),
        P(),
        P(),
        P(),
        P("fsdp", None),
        P(),
        P("fsdp", None),
        P(),
        P(("dp", "fsdp"), "ctx", None),
    )
    out_specs = (
        P(("dp", "fsdp"), "ctx", None),
        P(("dp", "fsdp"), "ctx", None),
        P(),
        P(),
        P(("dp", "fsdp"), "ctx"),
        P(),
        P(),
        P(("dp", "fsdp"), "ctx"),
        P(),
        P(),
        P(),
        P(("dp", "fsdp"), "ctx"),
        P(),
        P(("dp", "fsdp"), "ctx"),
        P(),
    )
    return jax.shard_map(
        make_body(mesh), mesh=mesh, in_specs=in_specs, out_specs=out_specs, check_vma=False)
```

```python
import math

import jax
import jax.numpy as jnp
from jax import lax
from jax.sharding import PartitionSpec as P

D = 1088
HEADS = 17
HEAD_DIM = 64
BLK = 64


EPSILON = 1e-05
NEGATIVE_FILL = -1e30


def normalize(values, gain, shift):
    center = values - jnp.mean(values, axis=-1, keepdims=True)
    inverse = lax.rsqrt(jnp.mean(center * center, axis=-1, keepdims=True) + EPSILON)
    normed = center * inverse
    return (normed, inverse, normed * gain + shift)


def normalize_back(incoming, normed, inverse, gain):
    gain_grad = jnp.sum(incoming * normed, axis=0)
    shift_grad = jnp.sum(incoming, axis=0)
    scaled = incoming * gain
    result = inverse * (
        scaled
        - jnp.mean(scaled, axis=-1, keepdims=True)
        - normed * jnp.mean(scaled * normed, axis=-1, keepdims=True)
    )
    return (result, gain_grad, shift_grad)


def gelu_pair(preact):
    normal_cdf = 0.5 * (1.0 + lax.erf(preact * (1.0 / math.sqrt(2.0))))
    density = jnp.exp(-0.5 * preact * preact) * (1.0 / math.sqrt(2.0 * math.pi))
    return (preact * normal_cdf, normal_cdf + preact * density)


def contract_rows(left, right):
    return lax.dot_general(
        left, right, (((0,), (0,)), ((), ())), preferred_element_type=jnp.float32
    )


def contract_cols(left, right):
    return lax.dot_general(
        left, right, (((1,), (1,)), ((), ())), preferred_element_type=jnp.float32
    )


def core_swap(array):
    return lax.ppermute(array, "fsdp", [(i, i ^ 1) for i in range(4)])


def chip_swap(array):
    return lax.ppermute(array, "fsdp", [(i, i ^ 2) for i in range(4)])


def gather_group(array):
    across = chip_swap(array)
    return jnp.concatenate([array, core_swap(array), across, core_swap(across)], axis=0)


def scatter_group(partial):
    own, near, far, diagonal = jnp.split(partial, 4, axis=0)
    received = core_swap(jnp.concatenate([near, diagonal], axis=0))
    count = own.shape[0]
    sent = (far + received[count:]).astype(jnp.bfloat16)
    return own + received[:count] + chip_swap(sent).astype(jnp.float32)


def exchange_columns(array, rank):
    width = array.shape[1] // 4
    pieces = []
    for step in range(4):
        piece = lax.dynamic_slice_in_dim(array, (rank ^ step) * width, width, 1)
        if step:
            piece = lax.ppermute(piece, "fsdp", [(i, i ^ step) for i in range(4)])
        pieces.append(piece)
    return pieces


def after(value, *others):
    return lax.optimization_barrier((value,) + others)[0]


def all_sum(array, mesh_axes):
    for axis, count in mesh_axes:
        bit = 1
        while bit < count:
            array = array + lax.ppermute(array, axis, [(i, i ^ bit) for i in range(count)])
            bit *= 2
    return array


def head_major(values):
    count = values.shape[0]
    return jnp.transpose(values.reshape(count, HEADS, HEAD_DIM), (1, 0, 2))


def row_major(values):
    count = values.shape[1]
    return jnp.transpose(values, (1, 0, 2)).reshape(count, HEADS * HEAD_DIM)


def make_body(mesh):
    n_dp, n_ctx, n_fsdp = mesh.shape["dp"], mesh.shape["ctx"], mesh.shape["fsdp"]
    paired = n_ctx == 2 and n_dp == 4

    def fetch_shards(shard, rank):
        rows = shard.shape[0]
        near = core_swap(shard)
        own = [(shard, rank * rows), (near, (rank ^ 1) * rows)]
        if not paired:
            across = chip_swap(shard)
            return own + [(across, (rank ^ 2) * rows), (core_swap(across), (rank ^ 3) * rows)], across
        side = lax.axis_index("ctx")
        part = rows // 24 * 8
        passed = chip_swap(lax.dynamic_slice_in_dim(shard, side * part, part, 0))
        direct = chip_swap(after(shard, passed)[2 * part :])
        other = ctx_swap(passed)
        pieces = [(passed, side * part), (direct, 2 * part), (other, (1 - side) * part)]
        far = [(value, (rank ^ 2) * rows + offset) for value, offset in pieces]
        far += [(core_swap(value), (rank ^ 3) * rows + offset) for value, offset in pieces]
        return own + far, direct

    def whole_matrix(pieces):
        width = pieces[0][0].shape[1]
        out = jnp.zeros((4 * pieces[0][0].shape[0], width), pieces[0][0].dtype)
        for value, offset in pieces:
            out = lax.dynamic_update_slice_in_dim(out, value, offset, 0)
        return out

    def gather_weight(shard, rank):
        rows = shard.shape[0]
        if paired:
            low = lax.axis_index("ctx") == 0
            passed = first = chip_swap(jnp.where(low, shard[: rows // 2], shard[rows // 2 :]))
            other = ctx_swap(passed)
            across = jnp.where(
                low,
                jnp.concatenate([passed, other], axis=0),
                jnp.concatenate([other, passed], axis=0),
            )
        else:
            across = first = chip_swap(shard)
        pieces = [shard, core_swap(shard), across, core_swap(across)]
        return whole_matrix([(v, (rank ^ i) * rows) for i, v in enumerate(pieces)]), first

    def plane_slices(array, width):
        order = range(4 * n_ctx)
        if paired:
            order = [4 * x + 2 * k + c for c in range(2) for x in range(2) for k in range(2)]
        return jnp.stack([array[:, i * width : (i + 1) * width] for i in order])

    def plane_rows(slices, rank_ctx, rank):
        slices = lax.all_to_all(slices, ("ctx", "fsdp"), 0, 0, tiled=True)
        return jnp.concatenate(
            [
                lax.dynamic_index_in_dim(
                    slices, (rank_ctx + s) % n_ctx * 4 + (rank ^ step), 0, keepdims=False
                )
                for step in range(4)
                for s in range(n_ctx)
            ],
            axis=0,
        )

    def line_start(product):
        if not paired:
            return product, None
        blocks = product.reshape(4, -1, product.shape[1])
        place = lax.axis_index("dp")
        sent = [lax.dynamic_index_in_dim(blocks, place ^ i, 0) for i in (1, 3)]
        kept = [lax.dynamic_index_in_dim(blocks, place ^ i, 0) for i in (0, 2)]
        sent = jnp.concatenate(sent, axis=0).astype(jnp.bfloat16)
        return kept, lax.ppermute(sent, "dp", [(i, i ^ 1) for i in range(4)])

    def line_middle(kept, received):
        if not paired:
            return kept, None
        sent = (kept[1][0] + received[1].astype(jnp.float32)).astype(jnp.bfloat16)
        last = lax.ppermute(sent, "dp", [(i, i ^ 2) for i in range(4)])
        return kept[0][0] + received[0].astype(jnp.float32), last

    def line_finish(total, rank, widths):
        if not paired:
            blocks = total.astype(jnp.bfloat16).reshape(n_dp * 4, -1, total.shape[1])
            blocks = lax.all_to_all(blocks, ("dp", "fsdp"), 0, 0, tiled=True)
            blocks = blocks.reshape((n_dp, 4) + blocks.shape[1:]).astype(jnp.float32)
            blocks = jnp.sum(blocks, axis=0)
            order = [blocks[i] for i in range(4)]
        else:
            total = total.astype(jnp.bfloat16)
            share = total.shape[0] // 4
            place = 2 * lax.axis_index("ctx") + rank % 2
            pieces = []
            for step in range(4):
                piece = lax.dynamic_slice_in_dim(total, (place ^ step) * share, share, 0)
                pairs = [
                    (4 * c + 2 * x + k, 4 * x + (2 * c + k ^ step))
                    for c in range(2)
                    for x in range(2)
                    for k in range(2)
                ]
                pieces.append(lax.ppermute(piece, ("ctx", "fsdp"), pairs).astype(jnp.float32))
            pieces = jnp.stack(pieces)
            order = [
                lax.dynamic_index_in_dim(pieces, (2 * h + k) ^ rank, 0, keepdims=False)
                for k in range(2)
                for h in range(2)
            ]
        shares, start = [], 0
        for width in widths:
            cut = slice(start, start + width)
            shares.append(jnp.concatenate([block[:, cut] for block in order], axis=1))
            start += width
        return shares

    def sides(array, rank_ctx):
        half = array.shape[1] // 2
        low, high = array[:, :half], array[:, half:]
        return jnp.where(rank_ctx == 0, low, high), jnp.where(rank_ctx == 0, high, low)

    def ctx_swap(array):
        return lax.ppermute(array, "ctx", [(0, 1), (1, 0)])

    def columns_start(left, right, rank_ctx):
        if not paired:
            return (left, right), None
        keep, give = sides(right, rank_ctx)
        return (left, keep), ctx_swap(contract_rows(left, give).astype(jnp.bfloat16))

    def columns_middle(kept, received):
        product = contract_rows(*kept)
        return product + received.astype(jnp.float32) if paired else product

    def columns_alone(product):
        rows, width = product.shape
        share = rows // (4 * n_dp)
        product = product.reshape(n_dp, 4, share, width)
        product = lax.all_to_all(product, "fsdp", 1, 3, tiled=True)
        product = product.reshape(n_dp * share, 4 * width)
        product = lax.psum_scatter(product, "dp", scatter_dimension=0, tiled=True)
        return lax.psum_scatter(product, "ctx", scatter_dimension=1, tiled=True)

    def rows_start(left, right, rank_ctx):
        if not paired:
            return (left, right), None
        keep, give = sides(right, rank_ctx)
        return (left, keep), contract_rows(left, give).astype(jnp.bfloat16)

    def rows_middle(kept, received):
        product = contract_rows(*kept)
        return product + received.astype(jnp.float32) if paired else product

    def rows_finish(total, last, rank):
        if not paired:
            rows, width = total.shape
            whole = jnp.zeros((4 * rows, width), jnp.float32)
            whole = lax.dynamic_update_slice_in_dim(whole, total, rank * rows, 0)
            whole = lax.psum_scatter(whole, ("dp", "fsdp"), scatter_dimension=0, tiled=True)
            return lax.psum_scatter(whole, "ctx", scatter_dimension=1, tiled=True)
        total = (total + last.astype(jnp.float32)).astype(jnp.bfloat16)
        pairs = [(4 * i + j, 4 * j + i) for i in range(4) for j in range(4)]
        return lax.ppermute(total, ("dp", "fsdp"), pairs).astype(jnp.float32)

    def layer(
        inputs,
        pair_table,
        first_gain,
        first_shift,
        proj_weight,
        query_bias,
        value_bias,
        mix_weight,
        mix_bias,
        second_gain,
        second_shift,
        up_weight,
        up_bias,
        down_weight,
        down_bias,
        output_grad,
    ):
        tokens = inputs[0]
        count = tokens.shape[0]
        incoming = output_grad[0]
        scale = 1.0 / math.sqrt(HEAD_DIM)
        rank_ctx, rank = lax.axis_index("ctx"), lax.axis_index("fsdp")

        shifts = range(1, n_ctx)
        all_tokens = jnp.concatenate(
            [tokens]
            + [lax.ppermute(tokens, "ctx", [(i, (i - s) % n_ctx) for i in range(n_ctx)]) for s in shifts],
            axis=0,
        )
        offsets = jnp.arange(BLK, dtype=jnp.int32)
        order = (rank_ctx + jnp.arange(n_ctx, dtype=jnp.int32)) % n_ctx
        key_pos = (pair_table[order][:, :, None] * BLK + offsets[None, None, :]).reshape(-1)
        query_pos = key_pos[:count]
        visible = query_pos[:, None] >= key_pos[None, :]

        proj_pieces, arrived = fetch_shards(proj_weight, rank)
        full_mix, arrived = gather_weight(after(mix_weight, arrived), rank)
        up_weight = after(up_weight, arrived)
        hidden_up = jnp.zeros((D, up_weight.shape[1] // 4), up_weight.dtype)
        for step, piece in enumerate(exchange_columns(up_weight, rank)):
            hidden_up = lax.dynamic_update_slice_in_dim(
                hidden_up, piece, (rank ^ step) * piece.shape[0], 0
            )
        hidden = hidden_up.shape[1]
        hidden_bias = lax.dynamic_slice_in_dim(up_bias, rank * hidden, hidden, 0)

        x_all = all_tokens.astype(jnp.float32)
        normed_all, inverse_all, scaled_all = normalize(x_all, first_gain, first_shift)
        first_all = scaled_all.astype(jnp.bfloat16)
        x_float, normed1, inverse1 = x_all[:count], normed_all[:count], inverse_all[:count]
        projected = 0.0
        for piece, offset in proj_pieces:
            columns = lax.dynamic_slice_in_dim(first_all, offset, piece.shape[0], 1)
            projected = projected + jnp.dot(columns, piece, preferred_element_type=jnp.float32)
        query = (projected[:count, :D] + query_bias).astype(jnp.bfloat16)
        keys = projected[:, D : 2 * D].astype(jnp.bfloat16)
        values = (projected[:, 2 * D :] + value_bias).astype(jnp.bfloat16)
        query_heads = head_major(query)
        key_heads = head_major(keys)
        value_heads = head_major(values)
        scores = (
            jnp.einsum("hqd,hkd->hqk", query_heads, key_heads, preferred_element_type=jnp.float32)
            * scale
        )
        masked = jnp.where(visible[None], scores, NEGATIVE_FILL)
        row_top = jnp.max(masked, axis=2, keepdims=True)
        log_total = row_top + jnp.log(
            jnp.sum(jnp.where(visible[None], jnp.exp(masked - row_top), 0.0), axis=2, keepdims=True)
        )
        probs_exact = jnp.where(visible[None], jnp.exp(masked - log_total), 0.0)
        probs_half = probs_exact.astype(jnp.bfloat16)
        attended_heads = jnp.einsum(
            "hqk,hkd->hqd", probs_half, value_heads, preferred_element_type=jnp.float32
        ).astype(jnp.bfloat16)
        attended = row_major(attended_heads)
        others = [
            lax.ppermute(attended, "ctx", [(i, (i - s) % n_ctx) for i in range(n_ctx)])
            for s in shifts
        ]
        all_attended = jnp.concatenate([attended] + others, axis=0)
        residual = (
            x_float + jnp.dot(attended, full_mix, preferred_element_type=jnp.float32) + mix_bias
        )
        normed2, inverse2, scaled_second = normalize(residual, second_gain, second_shift)
        second_in = scaled_second.astype(jnp.bfloat16)

        group_upstream = gather_group(after(incoming, arrived).astype(jnp.bfloat16))
        group_second = gather_group(after(second_in, *others))
        up_pre = jnp.dot(group_second, hidden_up, preferred_element_type=jnp.float32) + hidden_bias
        activation, slope = gelu_pair(up_pre)
        activation_half = activation.astype(jnp.bfloat16)
        up_grad = contract_cols(group_upstream, down_weight) * slope
        up_half = up_grad.astype(jnp.bfloat16)
        down_kept, down_given = rows_start(activation_half, group_upstream, rank_ctx)
        if paired:
            up_half = after(up_half, down_given)
            down_given = ctx_swap(down_given)
        second_part = contract_cols(up_half, hidden_up)
        second_back = scatter_group(second_part)
        residual_part, second_gain_part, second_shift_part = normalize_back(
            second_back, normed2, inverse2, second_gain
        )
        residual_grad = incoming + residual_part
        residual_half = residual_grad.astype(jnp.bfloat16)
        attended_grad = contract_cols(residual_half, full_mix).astype(jnp.bfloat16)
        group_rows = gather_group(
            after(jnp.concatenate([first_all, all_attended], axis=0), attended_grad)
        )
        group_rows = jnp.split(group_rows, 8, axis=0)
        group_first = jnp.concatenate(group_rows[::2], axis=0)
        group_attended = jnp.concatenate(group_rows[1::2], axis=0)
        mix_width, proj_width = D // (4 * n_ctx), 3 * D // (4 * n_ctx)
        grad_heads = head_major(attended_grad)
        delta = jnp.einsum(
            "hqd,hqd->hq", grad_heads, attended_heads, preferred_element_type=jnp.float32
        )
        prob_grad = jnp.einsum(
            "hqd,hkd->hqk", grad_heads, value_heads, preferred_element_type=jnp.float32
        )
        score_grad = (probs_exact * (prob_grad - delta[:, :, None]) * scale).astype(jnp.bfloat16)
        query_grad = row_major(
            jnp.einsum("hqk,hkd->hqd", score_grad, key_heads, preferred_element_type=jnp.float32)
        )
        key_part = row_major(
            jnp.einsum("hqk,hqd->hkd", score_grad, query_heads, preferred_element_type=jnp.float32)
        )
        value_part = row_major(
            jnp.einsum("hqk,hqd->hkd", probs_half, grad_heads, preferred_element_type=jnp.float32)
        )
        parts = jnp.concatenate([key_part, value_part], axis=1).reshape(n_ctx, count, 2 * D)
        key_value_grad = parts[0]
        for s in shifts:
            sent = parts[s].astype(jnp.bfloat16)
            key_value_grad = key_value_grad + lax.ppermute(
                sent, "ctx", [(i, (i + s) % n_ctx) for i in range(n_ctx)]
            ).astype(jnp.float32)
        if paired:
            down_given = after(down_given, sent)
        wide_kept, wide_received = columns_start(
            after(group_second, down_given) if paired else group_second, up_half, rank_ctx
        )
        down_kept, down_line = line_start(rows_middle(down_kept, down_given))
        full_proj = whole_matrix(
            [(after(proj_pieces[0][0], key_value_grad), proj_pieces[0][1])] + proj_pieces[1:]
        )
        proj_grad = jnp.concatenate([query_grad, key_value_grad], axis=1)
        proj_half = proj_grad.astype(jnp.bfloat16)
        slices = jnp.concatenate(
            [plane_slices(proj_half, proj_width), plane_slices(residual_half, mix_width)], axis=2
        )
        outputs = (
            residual
            + scatter_group(
                jnp.dot(
                    after(activation_half, slices), down_weight, preferred_element_type=jnp.float32
                )
            )
            + down_bias
        )
        if paired:
            down_line = after(down_line, slices)
        down_total, down_last = line_middle(down_kept, down_line)
        plane_grad = plane_rows(slices, rank_ctx, rank)
        proj_product = jnp.concatenate(
            [
                contract_rows(group_first, plane_grad[:, :proj_width]),
                contract_rows(group_attended, plane_grad[:, proj_width:]),
            ],
            axis=1,
        )
        proj_kept, proj_line = line_start(proj_product)
        if paired:
            down_last = after(down_last, proj_product)
        down_share = rows_finish(down_total, down_last, rank)
        first_back = contract_cols(proj_half, full_proj)
        input_part, first_gain_part, first_shift_part = normalize_back(
            first_back, normed1, inverse1, first_gain
        )
        input_grad = residual_grad + input_part

        axes = (("dp", n_dp), ("ctx", n_ctx), ("fsdp", n_fsdp))
        up_bias_part = lax.dynamic_update_slice_in_dim(
            jnp.zeros(up_bias.shape, jnp.float32), jnp.sum(up_grad, axis=0), rank * hidden, 0
        )
        sums = jnp.concatenate(
            [
                first_gain_part,
                first_shift_part,
                jnp.sum(query_grad, axis=0),
                jnp.sum(key_value_grad[:, D:], axis=0),
                jnp.sum(residual_grad, axis=0),
                second_gain_part,
                second_shift_part,
                jnp.sum(incoming, axis=0),
                up_bias_part,
            ]
        )
        sums = all_sum(sums, axes)
        if paired:
            wide_received = after(wide_received, sums)
        wide = columns_middle(wide_kept, wide_received)
        wide_kept, wide_line = line_start(wide)
        wide_total, wide_last = line_middle(wide_kept, wide_line)
        proj_total, proj_last = line_middle(proj_kept, proj_line)
        if paired:
            wide_total = wide_total + wide_last.astype(jnp.float32)
            proj_total = proj_total + proj_last.astype(jnp.float32)
            up_share, proj_share, mix_share = line_finish(
                jnp.concatenate([wide_total, proj_total], axis=1),
                rank,
                (hidden // 2, proj_width, mix_width),
            )
        else:
            up_share = columns_alone(wide)
            proj_share, mix_share = line_finish(proj_total, rank, (proj_width, mix_width))
        vectors = [sums[i * D : (i + 1) * D] for i in range(8)] + [sums[8 * D :]]
        return (
            outputs[None],
            input_grad[None],
            vectors[0],
            vectors[1],
            proj_share,
            vectors[2],
            vectors[3],
            mix_share,
            vectors[4],
            vectors[5],
            vectors[6],
            up_share,
            vectors[8],
            down_share,
            vectors[7],
        )

    return layer


def solution(mesh):
    in_specs = (
        P(("dp", "fsdp"), "ctx", None),
        P(),
        P(),
        P(),
        P("fsdp", None),
        P(),
        P(),
        P("fsdp", None),
        P(),
        P(),
        P(),
        P("fsdp", None),
        P(),
        P("fsdp", None),
        P(),
        P(("dp", "fsdp"), "ctx", None),
    )
    out_specs = (
        P(("dp", "fsdp"), "ctx", None),
        P(("dp", "fsdp"), "ctx", None),
        P(),
        P(),
        P(("dp", "fsdp"), "ctx"),
        P(),
        P(),
        P(("dp", "fsdp"), "ctx"),
        P(),
        P(),
        P(),
        P(("dp", "fsdp"), "ctx"),
        P(),
        P(("dp", "fsdp"), "ctx"),
        P(),
    )
    return jax.shard_map(
        make_body(mesh), mesh=mesh, in_specs=in_specs, out_specs=out_specs, check_vma=False)
```
